512 devices in a mesh: section: 8 (over y_hi, x), seq: 64 (over y_lo, z, core).
Axes of the slice: x: 4, y: 4 (y_hi: 2, y_lo: 2; y = y_hi * 2 + y_lo), z: 16, core: 2. Of those that a mesh axis runs over, the one named last changes fastest.
Arguments:
- cotangent: bfloat16 [8192, 4096], P('seq'), may hold values from -6 to 6
- in_gate: bfloat16 [8, 8192, 4096], P('section', 'seq'), may hold values from -4 to 4
- mid_gate: bfloat16 [8, 8192, 4096], P('section', 'seq'), may hold values from -4 to 4
- layer_inputs: bfloat16 [8, 8192, 4096], P('section', 'seq'), may hold values from -6 to 6
- filters: bfloat16 [8, 128, 256], P('section'), may hold values from -0.5 to 0.5
- steer_second: float32 [8, 4096], P('section', 'seq'), may hold values from 8192 to 131072
- filter_second: float32 [8, 128, 256], P('section', None, 'seq'), may hold values from 32768 to 524288
Outputs:
- steer_step: float32 [8, 4096], P('section', 'seq')
- filter_step: float32 [8, 128, 256], P('section', None, 'seq')
The draws below stay inside these ranges and needn't reach their ends.
All inputs are finite; a program needn't handle non-finite values.
Results may differ from the reference program's by a relative error of at most 0.0095.
Values may be sent and summed in bfloat16 or wider, within the bound.
A program may use at most 192 MiB of HBM per device.

```python
import math
import jax
import jax.numpy as jnp
from jax import lax

CHANNELS = 4096
GROUPS = 256
FILTER_LEN = 128
TOKENS = 8192
SECTIONS = 8


def block_scale(key, extent, cuts, least, largest):
    factor_of = 1.0
    for axis_at, shards_of in cuts:
        draws = jax.random.uniform(jax.random.fold_in(jax.random.fold_in(key, 6), axis_at), (shards_of,), jnp.float32, least / len(cuts), largest / len(cuts))
        factor_of = factor_of * jnp.repeat(jnp.exp(draws), extent[axis_at] // shards_of).reshape((-1,) + (1,) * (len(extent) - 1 - axis_at))
    return factor_of


def gaussian(own_key, extent, spread, reach, cuts=(), kind=jnp.bfloat16):
    level = block_scale(own_key, extent, cuts, -0.22, 0.18) if cuts else 1.0
    array = jax.random.normal(own_key, extent, jnp.float32) * spread * level
    return jnp.minimum(jnp.maximum(array, -reach), reach).astype(kind)


def setup_inputs(seed: int = 0) -> dict:
    key_of = jax.random.split(jax.random.key(seed), 8)
    return {
        "cotangent": gaussian(key_of[0], (TOKENS, CHANNELS), 1.0, 6.0, ((0, 64),)),
        "in_gate": gaussian(key_of[1], (SECTIONS, TOKENS, CHANNELS), 0.7, 4.0, ((0, 8), (1, 64))),
        "mid_gate": gaussian(key_of[2], (SECTIONS, TOKENS, CHANNELS), 0.7, 4.0, ((0, 8), (1, 64))),
        "layer_inputs": gaussian(key_of[3], (SECTIONS, TOKENS, CHANNELS), 1.0, 6.0, ((0, 8), (1, 64))),
        "filters": gaussian(key_of[4], (SECTIONS, FILTER_LEN, GROUPS), FILTER_LEN ** -0.5, 0.5, ((0, 8),)),
        "steer_second": jnp.clip(jnp.exp(math.log(131072.0) - 2.7725887 * jax.random.uniform(key_of[5], (SECTIONS, CHANNELS), jnp.float32) ** block_scale(key_of[5], (SECTIONS, CHANNELS), ((0, 8), (1, 64)), -0.2, 0.2)), 8192.0, 131072.0),
        "filter_second": jnp.clip(jnp.exp(math.log(524288.0) - 2.7725887 * jax.random.uniform(key_of[6], (SECTIONS, FILTER_LEN, GROUPS), jnp.float32) ** block_scale(key_of[6], (SECTIONS, FILTER_LEN, GROUPS), ((0, 8), (2, 64)), -0.2, 0.2)), 32768.0, 524288.0),
    }


def band_matrix(kernel, block_rows):
    filt_len, group_count = kernel.shape
    span_len = block_rows + filt_len
    padded = jnp.concatenate([kernel.T, jnp.zeros((group_count, block_rows + 1), kernel.dtype)], 1)
    tiled_rows = jnp.tile(padded, (1, block_rows))[:, :block_rows * span_len]
    return tiled_rows.reshape(group_count, block_rows, span_len)

def filter_rows(band_full, extended, row_count, filt_len, block_rows):
    group_count = band_full.shape[0]
    channel_count = extended.shape[1]
    group_size = channel_count // group_count
    block_count = row_count // block_rows
    summed = jnp.zeros((block_count, block_rows, group_count, group_size), jnp.float32)
    for part_index in range(filt_len // block_rows + 1):
        start = part_index * block_rows
        window_part = extended[start:start + row_count].astype(jnp.float32).reshape(block_count, block_rows, group_count, group_size)
        band_part = band_full[:, :, start:start + block_rows].astype(jnp.float32)
        summed = summed + jnp.einsum('grs,bsgc->brgc', band_part, window_part, precision=lax.Precision.HIGHEST)
    return summed.reshape(row_count, channel_count)

def filter_grad(extended, values, group_count, filt_len, block_rows):
    row_count, channel_count = values.shape
    group_size = channel_count // group_count
    block_count = row_count // block_rows
    span_len = block_rows + filt_len
    left_side = values.astype(jnp.float32).reshape(block_count, block_rows, group_count, group_size)
    pieces = []
    for part_index in range(filt_len // block_rows + 1):
        start = part_index * block_rows
        window_part = extended[start:start + row_count].astype(jnp.float32).reshape(block_count, block_rows, group_count, group_size)
        pieces.append(jnp.einsum('brgc,bsgc->grs', left_side, window_part, precision=lax.Precision.HIGHEST))
    pairwise = jnp.concatenate(pieces, 2)
    flat_rows = pairwise.reshape(group_count, block_rows * span_len)
    flat_rows = jnp.concatenate([flat_rows, jnp.zeros((group_count, block_rows), jnp.float32)], 1)
    skewed = flat_rows.reshape(group_count, block_rows, span_len + 1)
    return lax.optimization_barrier(jnp.sum(skewed[:, :, :filt_len], 1)).T

def reference(cotangent, in_gate, mid_gate, layer_inputs, filters, steer_second, filter_second):
    block_rows = math.gcd(32, FILTER_LEN)
    incoming = cotangent
    steer_steps = [None] * SECTIONS
    filter_steps = [None] * SECTIONS
    for layer_index in range(SECTIONS - 1, -1, -1):
        gate_now = in_gate[layer_index].astype(jnp.float32)
        mid_now = mid_gate[layer_index].astype(jnp.float32)
        values = (mid_now * layer_inputs[layer_index].astype(jnp.float32)).astype(jnp.bfloat16)
        weighted = (gate_now * incoming.astype(jnp.float32)).astype(jnp.bfloat16)
        extended = jnp.concatenate([weighted, jnp.zeros((FILTER_LEN, CHANNELS), jnp.bfloat16)], 0)
        band_full = band_matrix(filters[layer_index], block_rows)
        filtered = filter_rows(band_full, extended, TOKENS, FILTER_LEN, block_rows)
        outgoing = (incoming.astype(jnp.float32) + mid_now * filtered).astype(jnp.bfloat16)
        local_filter = filter_grad(extended, values, GROUPS, FILTER_LEN, block_rows)
        local_steer = lax.optimization_barrier(jnp.sum(outgoing.astype(jnp.float32), 0))
        steer_steps[layer_index] = local_steer / jnp.sqrt(steer_second[layer_index] + local_steer * local_steer)
        filter_steps[layer_index] = local_filter / jnp.sqrt(filter_second[layer_index] + local_filter * local_filter)
        incoming = outgoing
    return (jnp.stack(steer_steps, 0), jnp.stack(filter_steps, 0))
```

```python
import functools

import jax
import jax.numpy as jnp
from jax import lax
from jax.experimental import pallas as pl
from jax.experimental.pallas import tpu as pltpu
from jax.sharding import PartitionSpec as P

MESH = pl.DeviceIdType.MESH
F32 = jnp.float32
BF16 = jnp.bfloat16
CORES = 2
Y_PARTS = 2
SPLITS = 4
WIDE = 256
GROUP = 16


def iota(shape, dim):
    return lax.broadcasted_iota(jnp.int32, shape, dim)


def kernel(
    sections, seqs,
    cot, in_gate, mid_gate, inputs, filters, out,
    in_all, mid_all, x_all, grad, taps_out, taps_all, toep, ext, rev,
    steer, msg, got, half_in, half_sum, y_in, y_sum, z_in,
    local_sem, a2a_send, a2a_recv, tap_send, tap_recv, halo_send, halo_recv,
    msg_send, msg_recv, core_sem, y_sem, z_send, z_recv,
):
    rows, channels = cot.shape
    mine = channels // sections
    blocks = mine // WIDE
    groups = mine // GROUP
    z_size = seqs // (CORES * Y_PARTS)
    me = lax.axis_index("section")
    q = lax.axis_index("seq")
    core = lax.rem(q, CORES)
    z = lax.rem(lax.div(q, CORES), z_size)
    y = lax.div(q, CORES * z_size)

    def section_peer(step):
        return lax.rem(me + step, sections)

    def z_peer(step):
        return lax.rem(z + step, z_size)

    def seq_at(y_at, z_at, core_at):
        return (y_at * z_size + z_at) * CORES + core_at

    core_peer = seq_at(y, z, 1 - core)
    y_peer = seq_at(1 - y, z, core)
    chip_peer = lax.rem(q + 2 * core - 1 + seqs, seqs)

    sources = (in_gate, mid_gate, inputs)
    targets = (in_all, mid_all, x_all)

    for a in range(3):
        pltpu.make_async_copy(
            sources[a].at[:, pl.ds(pl.multiple_of(me * mine, 128), mine)],
            targets[a].at[me],
            a2a_recv.at[a, me],
        ).start()
    cot_copy = pltpu.make_async_copy(
        cot.at[:, pl.ds(pl.multiple_of(me * mine, 128), mine)], grad, local_sem.at[0]
    )
    cot_copy.start()

    barrier = pltpu.get_barrier_semaphore()
    peers = [(section_peer(d), q) for d in range(1, sections)]
    peers += [(me, core_peer), (me, y_peer), (me, chip_peer)]
    peers += [(me, seq_at(y, z_peer(d), core)) for d in range(1, z_size)]
    for peer in peers:
        pl.semaphore_signal(barrier, inc=1, device_id=peer, device_id_type=MESH)

    taps_t = filters[...].astype(F32).T.astype(BF16)
    for s in range(sections):
        taps_out[s] = taps_t[s * groups : (s + 1) * groups]
    filt_len = taps_out.shape[2]

    @pl.when(q == seqs - 1)
    def _():
        for l in range(sections):
            ext[l, rows : 2 * rows, :] = jnp.zeros((rows, mine), BF16)

    for l in range(sections):
        ext[l, 2 * rows : 3 * rows, :] = jnp.zeros((rows, mine), BF16)
    toep_row = iota((rows, filt_len), 0)
    toep_col = iota((rows, filt_len), 1)
    part = rows // SPLITS
    rev_row, rev_col = iota((rows, rows), 0), iota((rows, rows), 1)
    rev[...] = jnp.where(
        rev_row // part * (2 * part) + part - 1 - rev_row == rev_col, 1.0, 0.0
    ).astype(BF16)

    pl.semaphore_wait(barrier, len(peers))

    def tap_copy(to, layer, step):
        return pltpu.make_async_remote_copy(
            src_ref=taps_out.at[to],
            dst_ref=taps_all.at[layer],
            send_sem=tap_send.at[step],
            recv_sem=tap_recv.at[layer],
            device_id=(to, q),
            device_id_type=MESH,
        )

    def a2a_copy(a, to, layer, step):
        return pltpu.make_async_remote_copy(
            src_ref=sources[a].at[:, pl.ds(pl.multiple_of(to * mine, 128), mine)],
            dst_ref=targets[a].at[layer],
            send_sem=a2a_send.at[a, step],
            recv_sem=a2a_recv.at[a, layer],
            device_id=(to, q),
            device_id_type=MESH,
        )

    pltpu.make_async_copy(taps_out.at[me], taps_all.at[me], tap_recv.at[me]).start()
    for d in range(1, sections):
        tap_copy(section_peer(d), me, d).start()
    for a in range(3):
        for d in range(1, sections):
            a2a_copy(a, section_peer(d), me, d).start()

    def wait_a2a(a, layer):
        a2a_copy(a, section_peer(1), layer, 0).wait_recv()

    def build_toep(layer):
        tap_copy(section_peer(1), layer, 0).wait_recv()
        taps = taps_all[layer].astype(F32)
        near = toep_col >= toep_row
        for g in range(groups):
            wide = jnp.broadcast_to(taps[g : g + 1, :], (rows, filt_len))
            turned = pltpu.roll(wide, 0, 1, stride=1, stride_axis=0)
            b, k = divmod(g, WIDE // GROUP)
            toep[b, k * rows : (k + 1) * rows, 0:rows] = jnp.where(near, turned, 0.0).astype(BF16)
            toep[b, k * rows : (k + 1) * rows, rows : 2 * rows] = jnp.where(
                near, 0.0, turned
            ).astype(BF16)

    def halo_copy(layer, b):
        cols = slice(b * WIDE, (b + 1) * WIDE)
        return pltpu.make_async_remote_copy(
            src_ref=ext.at[layer, 0:rows, cols],
            dst_ref=ext.at[layer, rows : 2 * rows, cols],
            send_sem=halo_send.at[layer, b],
            recv_sem=halo_recv.at[layer, b],
            device_id=(me, lax.rem(q + seqs - 1, seqs)),
            device_id_type=MESH,
        )

    def weigh(layer, b):
        cols = slice(b * WIDE, (b + 1) * WIDE)
        ext[layer, 0:rows, cols] = (
            in_all[layer, :, cols].astype(F32) * grad[:, cols].astype(F32)
        ).astype(BF16)

        @pl.when(q > 0)
        def _():
            halo_copy(layer, b).start()

    lane_group = iota((rows, WIDE), 1) // GROUP

    def advance(layer, b):
        cols = slice(b * WIDE, (b + 1) * WIDE)

        @pl.when(q < seqs - 1)
        def _():
            halo_copy(layer, b).wait_recv()

        window = ext[layer, 0 : 2 * rows, cols]
        filtered = jnp.zeros((rows, WIDE), F32)
        for k in range(WIDE // GROUP):
            full = jnp.dot(
                toep[b, k * rows : (k + 1) * rows, :], window, preferred_element_type=F32
            )
            filtered = jnp.where(lane_group == k, full, filtered)
        fresh = (
            grad[:, cols].astype(F32) + mid_all[layer, :, cols].astype(F32) * filtered
        ).astype(BF16)
        grad[:, cols] = fresh
        steer[0:1, cols] = jnp.sum(fresh.astype(F32), 0, keepdims=True)

    part_col = iota((part, filt_len), 1)
    part_row = part - 1 - iota((part, filt_len), 0)
    part_near = part_col >= part_row
    split_lane = lax.rem(iota((part, SPLITS * 128), 1), 128) // GROUP

    def msg_copy(layer):
        return pltpu.make_async_remote_copy(
            src_ref=msg.at[layer],
            dst_ref=got.at[pl.ds(me * (mine // 128), mine // 128)],
            send_sem=msg_send.at[layer],
            recv_sem=msg_recv.at[me],
            device_id=(layer, q),
            device_id_type=MESH,
        )

    def filter_sums(layer):
        wait_a2a(2, layer)
        values = (mid_all[layer].astype(F32) * x_all[layer].astype(F32)).astype(BF16)
        turned = jnp.dot(rev[...], values, preferred_element_type=F32).astype(BF16)
        for c in range(mine // 128):
            cols = slice(c * 128, (c + 1) * 128)
            left = jnp.concatenate(
                [turned[s * part : (s + 1) * part, cols] for s in range(SPLITS)], 1
            )
            right = jnp.concatenate(
                [ext[layer, s * part : s * part + 2 * rows, cols] for s in range(SPLITS)], 1
            )
            stack = jnp.concatenate(
                [jnp.where(split_lane == k, left, jnp.zeros_like(left)) for k in range(8)], 0
            )
            pairs = lax.dot_general(
                stack, right, (((1,), (1,)), ((), ())), preferred_element_type=F32
            )
            lines = []
            for k in range(8):
                own = pairs[k * part : (k + 1) * part]
                folded = jnp.where(part_near, own[:, :filt_len], own[:, filt_len:])
                moved = pltpu.roll(
                    folded, (filt_len + 1 - part) % filt_len, 1, stride=1, stride_axis=0
                )
                lines.append(jnp.sum(moved, 0, keepdims=True))
            tail = [steer[0:1, cols], jnp.zeros((3, 128), F32)]
            msg[layer, c, 0] = jnp.concatenate(lines[:4] + tail, 0)
            msg[layer, c, 1] = jnp.concatenate(lines[4:] + tail, 0)

        @pl.when(layer != me)
        def _():
            msg_copy(layer).start()

        @pl.when(layer == me)
        def _():
            pltpu.make_async_copy(
                msg.at[layer],
                got.at[pl.ds(me * (mine // 128), mine // 128)],
                msg_recv.at[me],
            ).start()

    last = sections - 1
    cot_copy.wait()
    wait_a2a(0, last)
    for b in range(blocks):
        weigh(last, b)
    build_toep(last)

    def one_layer(turn, carry):
        layer = last - turn
        wait_a2a(1, layer)

        @pl.when(layer > 0)
        def _():
            wait_a2a(0, jnp.maximum(layer - 1, 0))

        for b in range(blocks):
            advance(layer, b)

            @pl.when(layer > 0)
            def _():
                weigh(jnp.maximum(layer - 1, 0), b)

        @pl.when(layer > 0)
        def _():
            build_toep(jnp.maximum(layer - 1, 0))

        filter_sums(layer)
        return carry

    lax.fori_loop(0, sections, one_layer, 0)

    per = mine // 128

    def wait_msg(j):
        pltpu.make_async_remote_copy(
            src_ref=msg.at[0],
            dst_ref=got.at[pl.ds(j * per, per)],
            send_sem=msg_send.at[0],
            recv_sem=msg_recv.at[j],
            device_id=(section_peer(1), q),
            device_id_type=MESH,
        ).wait_recv()

    for j in range(sections):
        wait_msg(j)
    core_copy = pltpu.make_async_remote_copy(
        src_ref=got.at[:, 1 - core],
        dst_ref=half_in,
        send_sem=core_sem.at[0],
        recv_sem=core_sem.at[1],
        device_id=(me, core_peer),
        device_id_type=MESH,
    )
    core_copy.start()
    core_copy.wait()
    half_sum[...] = got[:, core] + half_in[...]
    y_copy = pltpu.make_async_remote_copy(
        src_ref=half_sum.at[pl.ds((1 - y) * z_size, z_size)],
        dst_ref=y_in,
        send_sem=y_sem.at[0],
        recv_sem=y_sem.at[1],
        device_id=(me, y_peer),
        device_id_type=MESH,
    )
    y_copy.start()
    y_copy.wait()
    y_sum[...] = half_sum[pl.ds(y * z_size, z_size)] + y_in[...]

    def z_copy(step):
        to = z_peer(step)
        return pltpu.make_async_remote_copy(
            src_ref=y_sum.at[to],
            dst_ref=z_in.at[z],
            send_sem=z_send.at[step],
            recv_sem=z_recv.at[z],
            device_id=(me, seq_at(y, to, core)),
            device_id_type=MESH,
        )

    for d in range(1, z_size):
        z_copy(d).start()
    total = y_sum[z]
    for d in range(1, z_size):
        origin = z_peer(d)
        pltpu.make_async_remote_copy(
            src_ref=y_sum.at[0],
            dst_ref=z_in.at[origin],
            send_sem=z_send.at[d],
            recv_sem=z_recv.at[origin],
            device_id=(me, core_peer),
            device_id_type=MESH,
        ).wait_recv()
    for d in range(1, z_size):
        total = total + z_in[z_peer(d)]
    out[...] = jnp.where(core == 1, pltpu.roll(total, 64, 1), total)
    out[0:4, :] = total[0:4]

    for d in range(1, sections):
        tap_copy(section_peer(d), me, d).wait_send()
        for a in range(3):
            a2a_copy(a, section_peer(d), me, d).wait_send()
    for d in range(1, z_size):
        z_copy(d).wait_send()

    def drain(layer, carry):
        for b in range(blocks):

            @pl.when(q > 0)
            def _():
                halo_copy(layer, b).wait_send()

        @pl.when(layer != me)
        def _():
            msg_copy(layer).wait_send()

        return carry

    lax.fori_loop(0, sections, drain, 0)


def adagrad(grad_part, second_part):
    return grad_part / jnp.sqrt(second_part + grad_part * grad_part)


def body(sections, seqs, cotangent, in_gate, mid_gate, layer_inputs, filters, steer_second, filter_second):
    rows, channels = cotangent.shape
    filt_len = filters.shape[1]
    mine = channels // sections
    groups = mine // GROUP
    z_size = seqs // (CORES * Y_PARTS)
    assert rows == filt_len == 128 and mine % WIDE == 0
    dma = pltpu.SemaphoreType.DMA
    any_spec = pl.BlockSpec(memory_space=pl.ANY)
    vmem_spec = pl.BlockSpec(memory_space=pltpu.VMEM)
    sums = pl.pallas_call(
        functools.partial(kernel, sections, seqs),
        out_shape=jax.ShapeDtypeStruct((8, 128), F32),
        in_specs=[any_spec] * 4 + [vmem_spec],
        out_specs=vmem_spec,
        scratch_shapes=[
            pltpu.VMEM((sections, rows, mine), BF16),
            pltpu.VMEM((sections, rows, mine), BF16),
            pltpu.VMEM((sections, rows, mine), BF16),
            pltpu.VMEM((rows, mine), BF16),
            pltpu.VMEM((sections, groups, filt_len), BF16),
            pltpu.VMEM((sections, groups, filt_len), BF16),
            pltpu.VMEM((mine // WIDE, WIDE // GROUP * rows, 2 * rows), BF16),
            pltpu.VMEM((sections, 3 * rows, mine), BF16),
            pltpu.VMEM((rows, rows), BF16),
            pltpu.VMEM((8, mine), F32),
            pltpu.VMEM((sections, mine // 128, 2, 8, 128), F32),
            pltpu.VMEM((seqs // 2, 2, 8, 128), F32),
            pltpu.VMEM((seqs // 2, 8, 128), F32),
            pltpu.VMEM((seqs // 2, 8, 128), F32),
            pltpu.VMEM((z_size, 8, 128), F32),
            pltpu.VMEM((z_size, 8, 128), F32),
            pltpu.VMEM((z_size, 8, 128), F32),
            dma((1,)),
            dma((3, sections)),
            dma((3, sections)),
            dma((sections,)),
            dma((sections,)),
            dma((sections, mine // WIDE)),
            dma((sections, mine // WIDE)),
            dma((sections,)),
            dma((sections,)),
            dma((2,)),
            dma((2,)),
            dma((z_size,)),
            dma((z_size,)),
        ],
        compiler_params=pltpu.CompilerParams(
            collective_id=0, has_side_effects=True, vmem_limit_bytes=48 * 2**20
        ),
    )(cotangent, in_gate[0], mid_gate[0], layer_inputs[0], filters[0])
    steer_part = sums[4:5, :64]
    filter_part = sums[0:4].T
    return (
        adagrad(steer_part, steer_second),
        adagrad(filter_part, filter_second[0])[None],
    )


def solution(mesh):
    in_specs = (
        P("seq", None),
        P("section", "seq", None),
        P("section", "seq", None),
        P("section", "seq", None),
        P("section", None, None),
        P("section", "seq"),
        P("section", None, "seq"),
    )
    out_specs = (P("section", "seq"), P("section", None, "seq"))
    step = functools.partial(body, mesh.shape["section"], mesh.shape["seq"])
    return jax.shard_map(step, mesh=mesh, in_specs=in_specs, out_specs=out_specs, check_vma=False)
```

```python
import functools

import jax
import jax.numpy as jnp
from jax import lax
from jax.experimental import pallas as pl
from jax.experimental.pallas import tpu as pltpu
from jax.sharding import PartitionSpec as P

MESH = pl.DeviceIdType.MESH
F32 = jnp.float32
BF16 = jnp.bfloat16
CORES = 2
Y_PARTS = 2
SPLITS = 4
WIDE = 256
GROUP = 16


def iota(shape, dim):
    return lax.broadcasted_iota(jnp.int32, shape, dim)


def kernel(
    sections, seqs,
    cot, in_gate, mid_gate, inputs, filters, out,
    in_all, mid_all, x_all, grad, taps_in, taps_out, taps_all, toep, ext, rev,
    steer, msg, got, near_sum, z_in,
    local_sem, a2a_send, a2a_recv, tap_send, tap_recv, halo_send, halo_recv,
    msg_send, msg_recv, z_send, z_recv,
):
    rows, channels = cot.shape
    mine = channels // sections
    blocks = mine // WIDE
    groups = mine // GROUP
    z_size = seqs // (CORES * Y_PARTS)
    me = lax.axis_index("section")
    q = lax.axis_index("seq")
    core = lax.rem(q, CORES)
    z = lax.rem(lax.div(q, CORES), z_size)
    y = lax.div(q, CORES * z_size)

    def section_peer(step):
        return lax.rem(me + step, sections)

    def z_peer(step):
        return lax.rem(z + step, z_size)

    def seq_at(y_at, z_at, core_at):
        return (y_at * z_size + z_at) * CORES + core_at

    chip_peer = lax.rem(q + 2 * core - 1 + seqs, seqs)

    parcels = []
    for b in range(blocks):
        parcels += [(in_gate, in_all, b * WIDE, WIDE), (mid_gate, mid_all, b * WIDE, WIDE)]
    parcels += [(inputs, x_all, b * WIDE, WIDE) for b in range(blocks)]
    gate_at = {("in", b): 2 * b for b in range(blocks)}
    gate_at.update({("mid", b): 2 * b + 1 for b in range(blocks)})
    gate_at.update({("x", b): 2 * blocks + b for b in range(blocks)})

    def parcel_ends(p, to, layer):
        source, target, first, width = parcels[p]
        start = pl.multiple_of(to * mine + first, 128)
        return source.at[:, pl.ds(start, width)], target.at[layer, :, first : first + width]

    tap_load = pltpu.make_async_copy(filters, taps_in, local_sem.at[1])
    tap_load.start()
    for p in range(len(parcels)):
        source, target = parcel_ends(p, me, me)
        pltpu.make_async_copy(source, target, a2a_recv.at[p, me]).start()
    cot_copy = pltpu.make_async_copy(
        cot.at[:, pl.ds(pl.multiple_of(me * mine, 128), mine)], grad, local_sem.at[0]
    )
    cot_copy.start()

    barrier = pltpu.get_barrier_semaphore()
    peers = [
        (section_peer(d), seq_at(lax.rem(y + dy, Y_PARTS), z, lax.rem(core + dc, CORES)))
        for d in range(sections)
        for dy in range(Y_PARTS)
        for dc in range(CORES)
        if d or dy or dc
    ]
    peers += [(me, chip_peer)]
    peers += [(me, seq_at(y, z_peer(d), core)) for d in range(1, z_size)]
    for peer in peers:
        pl.semaphore_signal(barrier, inc=1, device_id=peer, device_id_type=MESH)

    tap_load.wait()
    taps_t = taps_in[...].astype(F32).T.astype(BF16)
    for s in range(sections):
        taps_out[s] = taps_t[s * groups : (s + 1) * groups]
    filt_len = taps_out.shape[2]

    @pl.when(q == seqs - 1)
    def _():
        for l in range(sections):
            ext[l, rows : 2 * rows, :] = jnp.zeros((rows, mine), BF16)

    for l in range(sections):
        ext[l, 2 * rows : 3 * rows, :] = jnp.zeros((rows, mine), BF16)
    toep_row = iota((rows, filt_len), 0)
    toep_col = iota((rows, filt_len), 1)
    part = rows // SPLITS
    rev_row, rev_col = iota((rows, rows), 0), iota((rows, rows), 1)
    rev[...] = jnp.where(
        rev_row // part * (2 * part) + part - 1 - rev_row == rev_col, 1.0, 0.0
    ).astype(BF16)

    pl.semaphore_wait(barrier, len(peers))

    def tap_copy(to, layer, step):
        return pltpu.make_async_remote_copy(
            src_ref=taps_out.at[to],
            dst_ref=taps_all.at[layer],
            send_sem=tap_send.at[step],
            recv_sem=tap_recv.at[layer],
            device_id=(to, q),
            device_id_type=MESH,
        )

    def a2a_copy(p, to, layer, step):
        source, target = parcel_ends(p, to, layer)
        return pltpu.make_async_remote_copy(
            src_ref=source,
            dst_ref=target,
            send_sem=a2a_send.at[p, step],
            recv_sem=a2a_recv.at[p, layer],
            device_id=(to, q),
            device_id_type=MESH,
        )

    pltpu.make_async_copy(taps_out.at[me], taps_all.at[me], tap_recv.at[me]).start()
    for d in range(1, sections):
        tap_copy(section_peer(d), me, d).start()
    for p in range(len(parcels)):
        for d in range(1, sections):
            a2a_copy(p, section_peer(d), me, d).start()

    def wait_a2a(p, layer):
        a2a_copy(p, section_peer(1), layer, 0).wait_recv()

    def build_toep(layer):
        tap_copy(section_peer(1), layer, 0).wait_recv()
        taps = taps_all[layer].astype(F32)
        near = toep_col >= toep_row
        for g in range(groups):
            wide = jnp.broadcast_to(taps[g : g + 1, :], (rows, filt_len))
            turned = pltpu.roll(wide, 0, 1, stride=1, stride_axis=0)
            b, k = divmod(g, WIDE // GROUP)
            toep[layer, b, k * rows : (k + 1) * rows, 0:rows] = jnp.where(near, turned, 0.0).astype(BF16)
            toep[layer, b, k * rows : (k + 1) * rows, rows : 2 * rows] = jnp.where(
                near, 0.0, turned
            ).astype(BF16)

    def halo_copy(layer, b):
        cols = slice(b * WIDE, (b + 1) * WIDE)
        return pltpu.make_async_remote_copy(
            src_ref=ext.at[layer, 0:rows, cols],
            dst_ref=ext.at[layer, rows : 2 * rows, cols],
            send_sem=halo_send.at[layer, b],
            recv_sem=halo_recv.at[layer, b],
            device_id=(me, lax.rem(q + seqs - 1, seqs)),
            device_id_type=MESH,
        )

    def weigh(layer, b):
        cols = slice(b * WIDE, (b + 1) * WIDE)
        wait_a2a(gate_at["in", b], layer)
        ext[layer, 0:rows, cols] = (
            in_all[layer, :, cols].astype(F32) * grad[:, cols].astype(F32)
        ).astype(BF16)

        @pl.when(q > 0)
        def _():
            halo_copy(layer, b).start()

    lane_group = iota((rows, WIDE), 1) // GROUP

    def advance(layer, b):
        cols = slice(b * WIDE, (b + 1) * WIDE)

        @pl.when(q < seqs - 1)
        def _():
            halo_copy(layer, b).wait_recv()

        window = ext[layer, 0 : 2 * rows, cols]
        filtered = jnp.zeros((rows, WIDE), F32)
        for k in range(WIDE // GROUP):
            full = jnp.dot(
                toep[layer, b, k * rows : (k + 1) * rows, :], window, preferred_element_type=F32
            )
            filtered = jnp.where(lane_group == k, full, filtered)
        wait_a2a(gate_at["mid", b], layer)
        fresh = (
            grad[:, cols].astype(F32) + mid_all[layer, :, cols].astype(F32) * filtered
        ).astype(BF16)
        grad[:, cols] = fresh
        steer[layer, :, cols] = jnp.sum(fresh.astype(F32), 0, keepdims=True)

    part_col = iota((part, filt_len), 1)
    part_row = part - 1 - iota((part, filt_len), 0)
    part_near = part_col >= part_row
    split_lane = lax.rem(iota((part, SPLITS * 128), 1), 128) // GROUP

    y_home = lax.div(me * Y_PARTS, sections)
    lane = lax.rem(me, sections // Y_PARTS)

    def msg_copy(layer, half):
        return pltpu.make_async_remote_copy(
            src_ref=msg.at[layer, half],
            dst_ref=got.at[lane, y, core],
            send_sem=msg_send.at[layer, half],
            recv_sem=msg_recv.at[lane, y, core],
            device_id=(layer, seq_at(y_home, z, half)),
            device_id_type=MESH,
        )

    def stays(layer, half):
        return jnp.logical_and(layer == me, jnp.logical_and(y_home == y, core == half))

    def filter_sums(layer, b):
        wide_cols = slice(b * WIDE, (b + 1) * WIDE)
        wait_a2a(gate_at["x", b], layer)
        values = (
            mid_all[layer, :, wide_cols].astype(F32) * x_all[layer, :, wide_cols].astype(F32)
        ).astype(BF16)
        turned = jnp.dot(rev[...], values, preferred_element_type=F32).astype(BF16)
        for inner in range(WIDE // 128):
            c = b * (WIDE // 128) + inner
            cols = slice(c * 128, (c + 1) * 128)
            own_cols = slice(inner * 128, (inner + 1) * 128)
            left = jnp.concatenate(
                [turned[s * part : (s + 1) * part, own_cols] for s in range(SPLITS)], 1
            )
            right = jnp.concatenate(
                [ext[layer, s * part : s * part + 2 * rows, cols] for s in range(SPLITS)], 1
            )
            stack = jnp.concatenate(
                [jnp.where(split_lane == k, left, jnp.zeros_like(left)) for k in range(8)], 0
            )
            pairs = lax.dot_general(
                stack, right, (((1,), (1,)), ((), ())), preferred_element_type=F32
            )
            lines = []
            for k in range(8):
                own = pairs[k * part : (k + 1) * part]
                folded = jnp.where(part_near, own[:, :filt_len], own[:, filt_len:])
                moved = pltpu.roll(
                    folded, (filt_len + 1 - part) % filt_len, 1, stride=1, stride_axis=0
                )
                lines.append(jnp.sum(moved, 0, keepdims=True))
            tail = [steer[layer, :, cols], jnp.zeros((3, 128), F32)]
            msg[layer, 0, c] = jnp.concatenate(lines[:4] + tail, 0)
            msg[layer, 1, c] = jnp.concatenate(lines[4:] + tail, 0)

    def send_sums(layer):
        for half in range(CORES):
            here = stays(layer, half)

            @pl.when(jnp.logical_not(here))
            def _():
                msg_copy(layer, half).start()

            @pl.when(here)
            def _():
                pltpu.make_async_copy(
                    msg.at[layer, half], got.at[lane, y, core], msg_recv.at[lane, y, core]
                ).start()

    last = sections - 1
    cot_copy.wait()

    def build_one(turn, carry):
        build_toep(last - turn)
        return carry

    lax.fori_loop(0, sections, build_one, 0)
    weigh(last, 0)

    def move(layer, b):
        advance(layer, b)

        @pl.when(layer > 0)
        def _():
            weigh(jnp.maximum(layer - 1, 0), b)

    def lead(turn, carry):
        move(last - turn, 0)
        return carry

    def sums_of(b):
        def sums(step, inner):
            filter_sums(last - step, b)
            if b == blocks - 1:
                send_sums(last - step)
            return inner

        return sums

    def trail(turn, carry):
        first, stop = 2 * (turn - 3), 2 * (turn - 2)
        lax.fori_loop(
            jnp.clip(first, 0, sections), jnp.clip(stop, 0, sections), sums_of(0), 0
        )
        lax.fori_loop(
            jnp.maximum(2 * (turn - last + 1), 0),
            jnp.clip(2 + (last - 2) * (turn - last + 1), 0, last),
            sums_of(1),
            0,
        )
        move(last - turn, 1)
        return carry

    lax.fori_loop(0, sections, lead, 0)
    weigh(last, 1)
    lax.fori_loop(0, sections, trail, 0)
    filter_sums(0, 1)
    send_sums(0)

    lanes = sections // Y_PARTS
    for j in range(lanes):
        chunk = jnp.zeros(got.shape[3:], F32)
        for dy in range(Y_PARTS):
            for dc in range(CORES):
                pltpu.make_async_remote_copy(
                    src_ref=msg.at[0, 0],
                    dst_ref=got.at[j, dy, dc],
                    send_sem=msg_send.at[0, 0],
                    recv_sem=msg_recv.at[j, dy, dc],
                    device_id=(section_peer(1), q),
                    device_id_type=MESH,
                ).wait_recv()
                chunk = chunk + got[j, dy, dc]
        near_sum[j * (mine // 128) : (j + 1) * (mine // 128)] = chunk

    def z_copy(step):
        to = z_peer(step)
        return pltpu.make_async_remote_copy(
            src_ref=near_sum.at[to],
            dst_ref=z_in.at[z],
            send_sem=z_send.at[step],
            recv_sem=z_recv.at[z],
            device_id=(me, seq_at(y, to, core)),
            device_id_type=MESH,
        )

    for d in range(1, z_size):
        z_copy(d).start()
    total = near_sum[z]
    for d in range(1, z_size):
        origin = z_peer(d)
        pltpu.make_async_remote_copy(
            src_ref=near_sum.at[0],
            dst_ref=z_in.at[origin],
            send_sem=z_send.at[d],
            recv_sem=z_recv.at[origin],
            device_id=(me, chip_peer),
            device_id_type=MESH,
        ).wait_recv()
    for d in range(1, z_size):
        total = total + z_in[z_peer(d)]
    out[...] = jnp.where(core == 1, pltpu.roll(total, 64, 1), total)
    out[0:4, :] = total[0:4]

    for d in range(1, sections):
        tap_copy(section_peer(d), me, d).wait_send()
        for p in range(len(parcels)):
            a2a_copy(p, section_peer(d), me, d).wait_send()
    for d in range(1, z_size):
        z_copy(d).wait_send()

    def drain(layer, carry):
        for b in range(blocks):

            @pl.when(q > 0)
            def _():
                halo_copy(layer, b).wait_send()

        for half in range(CORES):

            @pl.when(jnp.logical_not(stays(layer, half)))
            def _():
                msg_copy(layer, half).wait_send()

        return carry

    lax.fori_loop(0, sections, drain, 0)


def adagrad(grad_part, second_part):
    return grad_part / jnp.sqrt(second_part + grad_part * grad_part)


def body(sections, seqs, cotangent, in_gate, mid_gate, layer_inputs, filters, steer_second, filter_second):
    rows, channels = cotangent.shape
    filt_len = filters.shape[1]
    mine = channels // sections
    groups = mine // GROUP
    z_size = seqs // (CORES * Y_PARTS)
    assert rows == filt_len == 128 and mine == 2 * WIDE
    dma = pltpu.SemaphoreType.DMA
    hbm_spec = pl.BlockSpec(memory_space=pltpu.HBM)
    vmem_spec = pl.BlockSpec(memory_space=pltpu.VMEM)
    sums = pl.pallas_call(
        functools.partial(kernel, sections, seqs),
        out_shape=jax.ShapeDtypeStruct((8, 128), F32),
        in_specs=[hbm_spec] * 5,
        out_specs=vmem_spec,
        scratch_shapes=[
            pltpu.VMEM((sections, rows, mine), BF16),
            pltpu.VMEM((sections, rows, mine), BF16),
            pltpu.VMEM((sections, rows, mine), BF16),
            pltpu.VMEM((rows, mine), BF16),
            pltpu.VMEM((filt_len, channels // GROUP), BF16),
            pltpu.VMEM((sections, groups, filt_len), BF16),
            pltpu.VMEM((sections, groups, filt_len), BF16),
            pltpu.VMEM((sections, mine // WIDE, WIDE // GROUP * rows, 2 * rows), BF16),
            pltpu.VMEM((sections, 3 * rows, mine), BF16),
            pltpu.VMEM((rows, rows), BF16),
            pltpu.VMEM((sections, 1, mine), F32),
            pltpu.VMEM((sections, CORES, mine // 128, 8, 128), F32),
            pltpu.VMEM((sections // Y_PARTS, Y_PARTS, CORES, mine // 128, 8, 128), F32),
            pltpu.VMEM((z_size, 8, 128), F32),
            pltpu.VMEM((z_size, 8, 128), F32),
            dma((2,)),
            dma((3 * mine // WIDE, sections)),
            dma((3 * mine // WIDE, sections)),
            dma((sections,)),
            dma((sections,)),
            dma((sections, mine // WIDE)),
            dma((sections, mine // WIDE)),
            dma((sections, CORES)),
            dma((sections // Y_PARTS, Y_PARTS, CORES)),
            dma((z_size,)),
            dma((z_size,)),
        ],
        compiler_params=pltpu.CompilerParams(
            collective_id=0, has_side_effects=True, vmem_limit_bytes=63 * 2**20
        ),
    )(cotangent, in_gate[0], mid_gate[0], layer_inputs[0], filters[0])
    steer_part = sums[4:5, :64]
    filter_part = sums[0:4].T
    return (
        adagrad(steer_part, steer_second),
        adagrad(filter_part, filter_second[0])[None],
    )


def solution(mesh):
    in_specs = (
        P("seq", None),
        P("section", "seq", None),
        P("section", "seq", None),
        P("section", "seq", None),
        P("section", None, None),
        P("section", "seq"),
        P("section", None, "seq"),
    )
    out_specs = (P("section", "seq"), P("section", None, "seq"))
    step = functools.partial(body, mesh.shape["section"], mesh.shape["seq"])
    return jax.shard_map(step, mesh=mesh, in_specs=in_specs, out_specs=out_specs, check_vma=False)
```

```python
import functools

import jax
import jax.numpy as jnp
from jax import lax
from jax.experimental import pallas as pl
from jax.experimental.pallas import tpu as pltpu
from jax.sharding import PartitionSpec as P

MESH = pl.DeviceIdType.MESH
F32 = jnp.float32
BF16 = jnp.bfloat16
CORES = 2
Y_PARTS = 2
SPLITS = 4
WIDE = 256
GROUP = 16


def iota(shape, dim):
    return lax.broadcasted_iota(jnp.int32, shape, dim)


def kernel(
    sections, seqs,
    cot, in_gate, mid_gate, inputs, filters, out,
    in_stage, mid_stage, x_stage, in_all, mid_all, x_all, grad, taps_in, taps_out, taps_all, toep, ext, rev,
    steer, msg, got, near_sum, z_in,
    local_sem, stage_sem, a2a_send, a2a_recv, tap_send, tap_recv, halo_send, halo_recv,
    msg_send, msg_recv, z_send, z_recv,
):
    rows, channels = cot.shape
    mine = channels // sections
    blocks = mine // WIDE
    groups = mine // GROUP
    z_size = seqs // (CORES * Y_PARTS)
    me = lax.axis_index("section")
    q = lax.axis_index("seq")
    core = lax.rem(q, CORES)
    z = lax.rem(lax.div(q, CORES), z_size)
    y = lax.div(q, CORES * z_size)

    row = sections // 2

    def section_peer(step):
        half = lax.rem(lax.div(me, row) + step // row, 2)
        return half * row + lax.rem(lax.rem(me, row) + step % row, row)

    def z_peer(step):
        return lax.rem(z + step, z_size)

    def seq_at(y_at, z_at, core_at):
        return (y_at * z_size + z_at) * CORES + core_at

    chip_peer = lax.rem(q + 2 * core - 1 + seqs, seqs)

    parcels = [(0, in_all, 0, mine), (1, mid_all, 0, mine), (2, x_all, 0, mine)]

    sources = (in_stage, mid_stage, x_stage)
    stage_loads = [
        [
            pltpu.make_async_copy(
                whole.at[pl.ds(part * 32, 32)], stage.at[pl.ds(part * 32, 32)], stage_sem.at[a]
            )
            for part in range(rows // 32)
        ]
        for a, (whole, stage) in enumerate(zip((in_gate, mid_gate, inputs), sources))
    ]

    def parcel_ends(p, to, layer):
        source, target, first, width = parcels[p]
        start = pl.multiple_of(to * mine + first, 128)
        return sources[source].at[:, pl.ds(start, width)], target.at[layer, :, first : first + width]

    tap_load = pltpu.make_async_copy(filters, taps_in, local_sem.at[1])
    tap_load.start()
    for a in range(3):
        for load in stage_loads[a]:
            load.start()
    for p, (a, all_layers, first, width) in enumerate(parcels):
        start = pl.multiple_of(me * mine + first, 128)
        pltpu.make_async_copy(
            (in_gate, mid_gate, inputs)[a].at[:, pl.ds(start, width)],
            all_layers.at[me, :, first : first + width],
            a2a_recv.at[p, me],
        ).start()
    cot_copy = pltpu.make_async_copy(
        cot.at[:, pl.ds(pl.multiple_of(me * mine, 128), mine)], grad, local_sem.at[0]
    )
    cot_copy.start()

    barrier = pltpu.get_barrier_semaphore()
    peers = [
        (section_peer(d), seq_at(lax.rem(y + dy, Y_PARTS), z, lax.rem(core + dc, CORES)))
        for d in range(sections)
        for dy in range(Y_PARTS)
        for dc in range(CORES)
        if d or dy or dc
    ]
    peers += [(me, chip_peer)]
    peers += [(me, seq_at(y, z_peer(d), core)) for d in range(1, z_size)]
    for peer in peers:
        pl.semaphore_signal(barrier, inc=1, device_id=peer, device_id_type=MESH)

    tap_load.wait()
    taps_t = taps_in[...].astype(F32).T.astype(BF16)
    for s in range(sections):
        taps_out[s] = taps_t[s * groups : (s + 1) * groups]
    filt_len = taps_out.shape[2]

    @pl.when(q == seqs - 1)
    def _():
        for l in range(sections):
            ext[l, rows : 2 * rows, :] = jnp.zeros((rows, mine), BF16)

    for l in range(sections):
        ext[l, 2 * rows : 3 * rows, :] = jnp.zeros((rows, mine), BF16)
    toep_row = iota((rows, filt_len), 0)
    toep_col = iota((rows, filt_len), 1)
    part = rows // SPLITS
    rev_row, rev_col = iota((rows, rows), 0), iota((rows, rows), 1)
    rev[...] = jnp.where(
        rev_row // part * (2 * part) + part - 1 - rev_row == rev_col, 1.0, 0.0
    ).astype(BF16)

    pl.semaphore_wait(barrier, len(peers))

    def tap_copy(to, layer, step):
        return pltpu.make_async_remote_copy(
            src_ref=taps_out.at[to],
            dst_ref=taps_all.at[layer],
            send_sem=tap_send.at[step],
            recv_sem=tap_recv.at[layer],
            device_id=(to, q),
            device_id_type=MESH,
        )

    def a2a_copy(p, to, layer, step):
        source, target = parcel_ends(p, to, layer)
        return pltpu.make_async_remote_copy(
            src_ref=source,
            dst_ref=target,
            send_sem=a2a_send.at[p, step],
            recv_sem=a2a_recv.at[p, layer],
            device_id=(to, q),
            device_id_type=MESH,
        )

    pltpu.make_async_copy(taps_out.at[me], taps_all.at[me], tap_recv.at[me]).start()
    for d in range(1, sections):
        tap_copy(section_peer(d), me, d).start()
    for a in range(3):
        for load in stage_loads[a]:
            load.wait()
    for p in range(2):
        for d in (*range(row, sections), *range(1, row)):
            a2a_copy(p, section_peer(d), me, d).start()

    def wait_a2a(p, layer):
        a2a_copy(p, section_peer(1), layer, 0).wait_recv()

    def build_toep(layer):
        tap_copy(section_peer(1), layer, 0).wait_recv()
        taps = taps_all[layer].astype(F32)
        near = toep_col >= toep_row
        for g in range(groups):
            wide = jnp.broadcast_to(taps[g : g + 1, :], (rows, filt_len))
            turned = pltpu.roll(wide, 0, 1, stride=1, stride_axis=0)
            b, k = divmod(g, WIDE // GROUP)
            toep[layer, b, k * rows : (k + 1) * rows, 0:rows] = jnp.where(near, turned, 0.0).astype(BF16)
            toep[layer, b, k * rows : (k + 1) * rows, rows : 2 * rows] = jnp.where(
                near, 0.0, turned
            ).astype(BF16)

    def halo_copy(layer, b):
        cols = slice(b * WIDE, (b + 1) * WIDE)
        return pltpu.make_async_remote_copy(
            src_ref=ext.at[layer, 0:rows, cols],
            dst_ref=ext.at[layer, rows : 2 * rows, cols],
            send_sem=halo_send.at[layer, b],
            recv_sem=halo_recv.at[layer, b],
            device_id=(me, lax.rem(q + seqs - 1, seqs)),
            device_id_type=MESH,
        )

    def weigh(layer, b):
        cols = slice(b * WIDE, (b + 1) * WIDE)
        if b == 0:
            wait_a2a(0, layer)
        ext[layer, 0:rows, cols] = (
            in_all[layer, :, cols].astype(F32) * grad[:, cols].astype(F32)
        ).astype(BF16)

        @pl.when(q > 0)
        def _():
            halo_copy(layer, b).start()

    lane_group = iota((rows, WIDE), 1) // GROUP

    def advance(layer, b):
        cols = slice(b * WIDE, (b + 1) * WIDE)

        @pl.when(q < seqs - 1)
        def _():
            halo_copy(layer, b).wait_recv()

        window = ext[layer, 0 : 2 * rows, cols]
        filtered = jnp.zeros((rows, WIDE), F32)
        for k in range(WIDE // GROUP):
            full = jnp.dot(
                toep[layer, b, k * rows : (k + 1) * rows, :], window, preferred_element_type=F32
            )
            filtered = jnp.where(lane_group == k, full, filtered)
        if b == 0:
            wait_a2a(1, layer)
        fresh = (
            grad[:, cols].astype(F32) + mid_all[layer, :, cols].astype(F32) * filtered
        ).astype(BF16)
        grad[:, cols] = fresh
        steer[layer, :, cols] = jnp.sum(fresh.astype(F32), 0, keepdims=True)

    part_col = iota((part, filt_len), 1)
    part_row = part - 1 - iota((part, filt_len), 0)
    part_near = part_col >= part_row
    split_lane = lax.rem(iota((part, SPLITS * 128), 1), 128) // GROUP

    y_home = lax.div(me * Y_PARTS, sections)
    lane = lax.rem(me, sections // Y_PARTS)

    def msg_copy(layer, half):
        return pltpu.make_async_remote_copy(
            src_ref=msg.at[layer, half],
            dst_ref=got.at[lane, y, core],
            send_sem=msg_send.at[layer, half],
            recv_sem=msg_recv.at[lane, y, core],
            device_id=(layer, seq_at(y_home, z, half)),
            device_id_type=MESH,
        )

    def stays(layer, half):
        return jnp.logical_and(layer == me, jnp.logical_and(y_home == y, core == half))

    def filter_sums(layer):
        wait_a2a(2, layer)
        values = (mid_all[layer].astype(F32) * x_all[layer].astype(F32)).astype(BF16)
        turned = jnp.dot(rev[...], values, preferred_element_type=F32).astype(BF16)
        for c in range(mine // 128):
            cols = slice(c * 128, (c + 1) * 128)
            left = jnp.concatenate(
                [turned[s * part : (s + 1) * part, cols] for s in range(SPLITS)], 1
            )
            right = jnp.concatenate(
                [ext[layer, s * part : s * part + 2 * rows, cols] for s in range(SPLITS)], 1
            )
            stack = jnp.concatenate(
                [jnp.where(split_lane == k, left, jnp.zeros_like(left)) for k in range(8)], 0
            )
            pairs = lax.dot_general(
                stack, right, (((1,), (1,)), ((), ())), preferred_element_type=F32
            )
            lines = []
            for k in range(8):
                own = pairs[k * part : (k + 1) * part]
                folded = jnp.where(part_near, own[:, :filt_len], own[:, filt_len:])
                moved = pltpu.roll(
                    folded, (filt_len + 1 - part) % filt_len, 1, stride=1, stride_axis=0
                )
                lines.append(jnp.sum(moved, 0, keepdims=True))
            tail = [steer[layer, :, cols], jnp.zeros((3, 128), F32)]
            msg[layer, 0, c] = jnp.concatenate(lines[:4] + tail, 0)
            msg[layer, 1, c] = jnp.concatenate(lines[4:] + tail, 0)

        for half in range(CORES):
            here = stays(layer, half)

            @pl.when(jnp.logical_not(here))
            def _():
                msg_copy(layer, half).start()

            @pl.when(here)
            def _():
                pltpu.make_async_copy(
                    msg.at[layer, half], got.at[lane, y, core], msg_recv.at[lane, y, core]
                ).start()

    last = sections - 1
    cot_copy.wait()

    def build_one(turn, carry):
        build_toep(last - turn)
        return carry

    lax.fori_loop(0, sections, build_one, 0)
    for b in range(blocks):
        weigh(last, b)

    def sums(step, carry):
        filter_sums(last - step)
        return carry

    def one_layer(turn, carry):
        @pl.when(turn == 0)
        def _():
            for d in range(row, sections):
                a2a_copy(2, section_peer(d), me, d).start()

        @pl.when(jnp.logical_and(turn > 0, turn < row))
        def _():
            step = jnp.clip(turn, 1, row - 1)
            a2a_copy(2, section_peer(step), me, step).start()

        late = 2 * (turn - 5)
        lax.fori_loop(jnp.maximum(late, 0), jnp.maximum(late + 2, 0), sums, 0)
        layer = last - turn
        for b in range(blocks):
            advance(layer, b)

            @pl.when(layer > 0)
            def _():
                weigh(jnp.maximum(layer - 1, 0), b)

        return carry

    lax.fori_loop(0, sections, one_layer, 0)
    lax.fori_loop(sections - 2, sections, sums, 0)

    lanes = sections // Y_PARTS
    for j in range(lanes):
        chunk = jnp.zeros(got.shape[3:], F32)
        for dy in range(Y_PARTS):
            for dc in range(CORES):
                pltpu.make_async_remote_copy(
                    src_ref=msg.at[0, 0],
                    dst_ref=got.at[j, dy, dc],
                    send_sem=msg_send.at[0, 0],
                    recv_sem=msg_recv.at[j, dy, dc],
                    device_id=(section_peer(1), q),
                    device_id_type=MESH,
                ).wait_recv()
                chunk = chunk + got[j, dy, dc]
        near_sum[j * (mine // 128) : (j + 1) * (mine // 128)] = chunk

    def z_copy(step):
        to = z_peer(step)
        return pltpu.make_async_remote_copy(
            src_ref=near_sum.at[to],
            dst_ref=z_in.at[z],
            send_sem=z_send.at[step],
            recv_sem=z_recv.at[z],
            device_id=(me, seq_at(y, to, core)),
            device_id_type=MESH,
        )

    for d in range(1, z_size):
        z_copy(d).start()
    total = near_sum[z]
    for d in range(1, z_size):
        origin = z_peer(d)
        pltpu.make_async_remote_copy(
            src_ref=near_sum.at[0],
            dst_ref=z_in.at[origin],
            send_sem=z_send.at[d],
            recv_sem=z_recv.at[origin],
            device_id=(me, chip_peer),
            device_id_type=MESH,
        ).wait_recv()
    for d in range(1, z_size):
        total = total + z_in[z_peer(d)]
    out[...] = jnp.where(core == 1, pltpu.roll(total, 64, 1), total)
    out[0:4, :] = total[0:4]

    for d in range(1, sections):
        tap_copy(section_peer(d), me, d).wait_send()
        for p in range(len(parcels)):
            a2a_copy(p, section_peer(d), me, d).wait_send()
    for d in range(1, z_size):
        z_copy(d).wait_send()

    def drain(layer, carry):
        for b in range(blocks):

            @pl.when(q > 0)
            def _():
                halo_copy(layer, b).wait_send()

        for half in range(CORES):

            @pl.when(jnp.logical_not(stays(layer, half)))
            def _():
                msg_copy(layer, half).wait_send()

        return carry

    lax.fori_loop(0, sections, drain, 0)


def adagrad(grad_part, second_part):
    return grad_part / jnp.sqrt(second_part + grad_part * grad_part)


def body(sections, seqs, cotangent, in_gate, mid_gate, layer_inputs, filters, steer_second, filter_second):
    rows, channels = cotangent.shape
    filt_len = filters.shape[1]
    mine = channels // sections
    groups = mine // GROUP
    z_size = seqs // (CORES * Y_PARTS)
    assert rows == filt_len == 128 and mine == 2 * WIDE
    dma = pltpu.SemaphoreType.DMA
    hbm_spec = pl.BlockSpec(memory_space=pltpu.HBM)
    vmem_spec = pl.BlockSpec(memory_space=pltpu.VMEM)
    sums = pl.pallas_call(
        functools.partial(kernel, sections, seqs),
        out_shape=jax.ShapeDtypeStruct((8, 128), F32),
        in_specs=[hbm_spec] * 5,
        out_specs=vmem_spec,
        scratch_shapes=[
            pltpu.VMEM((rows, channels), BF16),
            pltpu.VMEM((rows, channels), BF16),
            pltpu.VMEM((rows, channels), BF16),
            pltpu.VMEM((sections, rows, mine), BF16),
            pltpu.VMEM((sections, rows, mine), BF16),
            pltpu.VMEM((sections, rows, mine), BF16),
            pltpu.VMEM((rows, mine), BF16),
            pltpu.VMEM((filt_len, channels // GROUP), BF16),
            pltpu.VMEM((sections, groups, filt_len), BF16),
            pltpu.VMEM((sections, groups, filt_len), BF16),
            pltpu.VMEM((sections, mine // WIDE, WIDE // GROUP * rows, 2 * rows), BF16),
            pltpu.VMEM((sections, 3 * rows, mine), BF16),
            pltpu.VMEM((rows, rows), BF16),
            pltpu.VMEM((sections, 1, mine), F32),
            pltpu.VMEM((sections, CORES, mine // 128, 8, 128), F32),
            pltpu.VMEM((sections // Y_PARTS, Y_PARTS, CORES, mine // 128, 8, 128), F32),
            pltpu.VMEM((z_size, 8, 128), F32),
            pltpu.VMEM((z_size, 8, 128), F32),
            dma((2,)),
            dma((3,)),
            dma((3, sections)),
            dma((3, sections)),
            dma((sections,)),
            dma((sections,)),
            dma((sections, mine // WIDE)),
            dma((sections, mine // WIDE)),
            dma((sections, CORES)),
            dma((sections // Y_PARTS, Y_PARTS, CORES)),
            dma((z_size,)),
            dma((z_size,)),
        ],
        compiler_params=pltpu.CompilerParams(
            collective_id=0, has_side_effects=True, vmem_limit_bytes=63 * 2**20
        ),
    )(cotangent, in_gate[0], mid_gate[0], layer_inputs[0], filters[0])
    steer_part = sums[4:5, :64]
    filter_part = sums[0:4].T
    return (
        adagrad(steer_part, steer_second),
        adagrad(filter_part, filter_second[0])[None],
    )


def solution(mesh):
    in_specs = (
        P("seq", None),
        P("section", "seq", None),
        P("section", "seq", None),
        P("section", "seq", None),
        P("section", None, None),
        P("section", "seq"),
        P("section", None, "seq"),
    )
    out_specs = (P("section", "seq"), P("section", None, "seq"))
    step = functools.partial(body, mesh.shape["section"], mesh.shape["seq"])
    return jax.shard_map(step, mesh=mesh, in_specs=in_specs, out_specs=out_specs, check_vma=False)
```

```python
import functools

import jax
import jax.numpy as jnp
from jax import lax
from jax.experimental import pallas as pl
from jax.experimental.pallas import tpu as pltpu
from jax.sharding import PartitionSpec as P

MESH = pl.DeviceIdType.MESH
F32 = jnp.float32
BF16 = jnp.bfloat16
CORES = 2
Y_PARTS = 2
SPLITS = 4
WIDE = 256
GROUP = 16


def iota(shape, dim):
    return lax.broadcasted_iota(jnp.int32, shape, dim)


def kernel(
    sections, seqs,
    cot, in_gate, mid_gate, inputs, filters, out,
    in_stage, mid_stage, x_stage, in_all, mid_all, x_all, grad, taps_in, taps_out, taps_all, toep, ext, rev,
    steer, msg, got, near_sum, z_in,
    local_sem, stage_sem, a2a_send, a2a_recv, tap_send, tap_recv, halo_send, halo_recv,
    msg_send, msg_recv, z_send, z_recv,
):
    rows, channels = cot.shape
    mine = channels // sections
    blocks = mine // WIDE
    groups = mine // GROUP
    z_size = seqs // (CORES * Y_PARTS)
    me = lax.axis_index("section")
    q = lax.axis_index("seq")
    core = lax.rem(q, CORES)
    z = lax.rem(lax.div(q, CORES), z_size)
    y = lax.div(q, CORES * z_size)

    row = sections // 2

    def section_peer(step):
        half = lax.rem(lax.div(me, row) + step // row, 2)
        return half * row + lax.rem(lax.rem(me, row) + step % row, row)

    def z_peer(step):
        return lax.rem(z + step, z_size)

    def seq_at(y_at, z_at, core_at):
        return (y_at * z_size + z_at) * CORES + core_at

    chip_peer = lax.rem(q + 2 * core - 1 + seqs, seqs)

    parcels = [(0, in_all, 0, mine), (1, mid_all, 0, mine), (2, x_all, 0, mine)]

    sources = (in_stage, mid_stage, x_stage)
    stage_loads = [
        [
            pltpu.make_async_copy(
                whole.at[pl.ds(part * 32, 32)], stage.at[pl.ds(part * 32, 32)], stage_sem.at[a]
            )
            for part in range(rows // 32)
        ]
        for a, (whole, stage) in enumerate(zip((in_gate, mid_gate, inputs), sources))
    ]

    def parcel_ends(p, to, layer):
        source, target, first, width = parcels[p]
        start = pl.multiple_of(to * mine + first, 128)
        return sources[source].at[:, pl.ds(start, width)], target.at[layer, :, first : first + width]

    tap_load = pltpu.make_async_copy(filters, taps_in, local_sem.at[1])
    tap_load.start()
    for a in range(3):
        for load in stage_loads[a]:
            load.start()
    for p, (a, all_layers, first, width) in enumerate(parcels):
        start = pl.multiple_of(me * mine + first, 128)
        pltpu.make_async_copy(
            (in_gate, mid_gate, inputs)[a].at[:, pl.ds(start, width)],
            all_layers.at[me, :, first : first + width],
            a2a_recv.at[p, me],
        ).start()
    cot_copy = pltpu.make_async_copy(
        cot.at[:, pl.ds(pl.multiple_of(me * mine, 128), mine)], grad, local_sem.at[0]
    )
    cot_copy.start()

    barrier = pltpu.get_barrier_semaphore()
    peers = [
        (section_peer(d), seq_at(lax.rem(y + dy, Y_PARTS), z, lax.rem(core + dc, CORES)))
        for d in range(sections)
        for dy in range(Y_PARTS)
        for dc in range(CORES)
        if d or dy or dc
    ]
    peers += [(me, chip_peer)]
    peers += [(me, seq_at(y, z_peer(d), core)) for d in range(1, z_size)]
    for peer in peers:
        pl.semaphore_signal(barrier, inc=1, device_id=peer, device_id_type=MESH)

    tap_load.wait()
    taps_t = taps_in[...].astype(F32).T.astype(BF16)
    for s in range(sections):
        taps_out[s] = taps_t[s * groups : (s + 1) * groups]
    filt_len = taps_out.shape[2]

    @pl.when(q == seqs - 1)
    def _():
        for l in range(sections):
            ext[l, rows : 2 * rows, :] = jnp.zeros((rows, mine), BF16)

    for l in range(sections):
        ext[l, 2 * rows : 3 * rows, :] = jnp.zeros((rows, mine), BF16)
    toep_row = iota((rows, filt_len), 0)
    toep_col = iota((rows, filt_len), 1)
    part = rows // SPLITS
    rev_row, rev_col = iota((rows, rows), 0), iota((rows, rows), 1)
    rev[...] = jnp.where(
        rev_row // part * (2 * part) + part - 1 - rev_row == rev_col, 1.0, 0.0
    ).astype(BF16)

    pl.semaphore_wait(barrier, len(peers))

    def tap_copy(to, layer, step):
        return pltpu.make_async_remote_copy(
            src_ref=taps_out.at[to],
            dst_ref=taps_all.at[layer],
            send_sem=tap_send.at[step],
            recv_sem=tap_recv.at[layer],
            device_id=(to, q),
            device_id_type=MESH,
        )

    def a2a_copy(p, to, layer, step):
        source, target = parcel_ends(p, to, layer)
        return pltpu.make_async_remote_copy(
            src_ref=source,
            dst_ref=target,
            send_sem=a2a_send.at[p, step],
            recv_sem=a2a_recv.at[p, layer],
            device_id=(to, q),
            device_id_type=MESH,
        )

    pltpu.make_async_copy(taps_out.at[me], taps_all.at[me], tap_recv.at[me]).start()
    for d in range(1, sections):
        tap_copy(section_peer(d), me, d).start()
    for a in range(3):
        for load in stage_loads[a]:
            load.wait()
    for p in range(2):
        for d in (*range(row, sections), *range(1, row)):
            a2a_copy(p, section_peer(d), me, d).start()

    @pl.when(me >= row)
    def _():
        for d in range(row, sections):
            a2a_copy(2, section_peer(d), me, d).start()

    def wait_a2a(p, layer):
        a2a_copy(p, section_peer(1), layer, 0).wait_recv()

    def build_toep(layer):
        tap_copy(section_peer(1), layer, 0).wait_recv()
        taps = taps_all[layer].astype(F32)
        near = toep_col >= toep_row
        for g in range(groups):
            wide = jnp.broadcast_to(taps[g : g + 1, :], (rows, filt_len))
            turned = pltpu.roll(wide, 0, 1, stride=1, stride_axis=0)
            b, k = divmod(g, WIDE // GROUP)
            toep[layer, b, k * rows : (k + 1) * rows, 0:rows] = jnp.where(near, turned, 0.0).astype(BF16)
            toep[layer, b, k * rows : (k + 1) * rows, rows : 2 * rows] = jnp.where(
                near, 0.0, turned
            ).astype(BF16)

    def halo_copy(layer, b):
        cols = slice(b * WIDE, (b + 1) * WIDE)
        return pltpu.make_async_remote_copy(
            src_ref=ext.at[layer, 0:rows, cols],
            dst_ref=ext.at[layer, rows : 2 * rows, cols],
            send_sem=halo_send.at[layer, b],
            recv_sem=halo_recv.at[layer, b],
            device_id=(me, lax.rem(q + seqs - 1, seqs)),
            device_id_type=MESH,
        )

    def weigh(layer, b):
        cols = slice(b * WIDE, (b + 1) * WIDE)
        if b == 0:
            wait_a2a(0, layer)
        ext[layer, 0:rows, cols] = (
            in_all[layer, :, cols].astype(F32) * grad[:, cols].astype(F32)
        ).astype(BF16)

        @pl.when(q > 0)
        def _():
            halo_copy(layer, b).start()

    lane_group = iota((rows, WIDE), 1) // GROUP

    def advance(layer, b):
        cols = slice(b * WIDE, (b + 1) * WIDE)

        @pl.when(q < seqs - 1)
        def _():
            halo_copy(layer, b).wait_recv()

        window = ext[layer, 0 : 2 * rows, cols]
        filtered = jnp.zeros((rows, WIDE), F32)
        for k in range(WIDE // GROUP):
            full = jnp.dot(
                toep[layer, b, k * rows : (k + 1) * rows, :], window, preferred_element_type=F32
            )
            filtered = jnp.where(lane_group == k, full, filtered)
        if b == 0:
            wait_a2a(1, layer)
        fresh = (
            grad[:, cols].astype(F32) + mid_all[layer, :, cols].astype(F32) * filtered
        ).astype(BF16)
        grad[:, cols] = fresh
        steer[layer, :, cols] = jnp.sum(fresh.astype(F32), 0, keepdims=True)

    part_col = iota((part, filt_len), 1)
    part_row = part - 1 - iota((part, filt_len), 0)
    part_near = part_col >= part_row
    split_lane = lax.rem(iota((part, SPLITS * 128), 1), 128) // GROUP

    y_home = lax.div(me * Y_PARTS, sections)
    lane = lax.rem(me, sections // Y_PARTS)

    def msg_copy(layer, half):
        return pltpu.make_async_remote_copy(
            src_ref=msg.at[layer, half],
            dst_ref=got.at[lane, y, core],
            send_sem=msg_send.at[layer, half],
            recv_sem=msg_recv.at[lane, y, core],
            device_id=(layer, seq_at(y_home, z, half)),
            device_id_type=MESH,
        )

    def stays(layer, half):
        return jnp.logical_and(layer == me, jnp.logical_and(y_home == y, core == half))

    def filter_sums(layer):
        wait_a2a(2, layer)
        values = (mid_all[layer].astype(F32) * x_all[layer].astype(F32)).astype(BF16)
        turned = jnp.dot(rev[...], values, preferred_element_type=F32).astype(BF16)
        for c in range(mine // 128):
            cols = slice(c * 128, (c + 1) * 128)
            left = jnp.concatenate(
                [turned[s * part : (s + 1) * part, cols] for s in range(SPLITS)], 1
            )
            right = jnp.concatenate(
                [ext[layer, s * part : s * part + 2 * rows, cols] for s in range(SPLITS)], 1
            )
            stack = jnp.concatenate(
                [jnp.where(split_lane == k, left, jnp.zeros_like(left)) for k in range(8)], 0
            )
            pairs = lax.dot_general(
                stack, right, (((1,), (1,)), ((), ())), preferred_element_type=F32
            )
            lines = []
            for k in range(8):
                own = pairs[k * part : (k + 1) * part]
                folded = jnp.where(part_near, own[:, :filt_len], own[:, filt_len:])
                moved = pltpu.roll(
                    folded, (filt_len + 1 - part) % filt_len, 1, stride=1, stride_axis=0
                )
                lines.append(jnp.sum(moved, 0, keepdims=True))
            tail = [steer[layer, :, cols], jnp.zeros((3, 128), F32)]
            msg[layer, 0, c] = jnp.concatenate(lines[:4] + tail, 0)
            msg[layer, 1, c] = jnp.concatenate(lines[4:] + tail, 0)

        for half in range(CORES):
            here = stays(layer, half)

            @pl.when(jnp.logical_not(here))
            def _():
                msg_copy(layer, half).start()

            @pl.when(here)
            def _():
                pltpu.make_async_copy(
                    msg.at[layer, half], got.at[lane, y, core], msg_recv.at[lane, y, core]
                ).start()

    last = sections - 1
    cot_copy.wait()

    def build_one(turn, carry):
        build_toep(last - turn)
        return carry

    lax.fori_loop(0, sections, build_one, 0)
    for b in range(blocks):
        weigh(last, b)

    def sums(step, carry):
        filter_sums(last - step)
        return carry

    def one_layer(turn, carry):
        @pl.when(jnp.logical_and(turn == 0, me < row))
        def _():
            for d in range(row, sections):
                a2a_copy(2, section_peer(d), me, d).start()

        @pl.when(jnp.logical_and(turn > 0, turn < row))
        def _():
            step = jnp.clip(turn, 1, row - 1)
            a2a_copy(2, section_peer(step), me, step).start()

        late = 2 * (turn - 4)
        lax.fori_loop(jnp.maximum(late, 0), jnp.clip(late + 2, 0, last), sums, 0)
        layer = last - turn
        for b in range(blocks):
            advance(layer, b)

            @pl.when(layer > 0)
            def _():
                weigh(jnp.maximum(layer - 1, 0), b)

        return carry

    lax.fori_loop(0, sections, one_layer, 0)
    filter_sums(0)

    lanes = sections // Y_PARTS
    for j in range(lanes):
        chunk = jnp.zeros(got.shape[3:], F32)
        for dy in range(Y_PARTS):
            for dc in range(CORES):
                pltpu.make_async_remote_copy(
                    src_ref=msg.at[0, 0],
                    dst_ref=got.at[j, dy, dc],
                    send_sem=msg_send.at[0, 0],
                    recv_sem=msg_recv.at[j, dy, dc],
                    device_id=(section_peer(1), q),
                    device_id_type=MESH,
                ).wait_recv()
                chunk = chunk + got[j, dy, dc]
        near_sum[j * (mine // 128) : (j + 1) * (mine // 128)] = chunk

    def z_copy(step):
        to = z_peer(step)
        return pltpu.make_async_remote_copy(
            src_ref=near_sum.at[to],
            dst_ref=z_in.at[z],
            send_sem=z_send.at[step],
            recv_sem=z_recv.at[z],
            device_id=(me, seq_at(y, to, core)),
            device_id_type=MESH,
        )

    for d in range(1, z_size):
        z_copy(d).start()
    total = near_sum[z]
    for d in range(1, z_size):
        origin = z_peer(d)
        pltpu.make_async_remote_copy(
            src_ref=near_sum.at[0],
            dst_ref=z_in.at[origin],
            send_sem=z_send.at[d],
            recv_sem=z_recv.at[origin],
            device_id=(me, chip_peer),
            device_id_type=MESH,
        ).wait_recv()
    for d in range(1, z_size):
        total = total + z_in[z_peer(d)]
    out[...] = jnp.where(core == 1, pltpu.roll(total, 64, 1), total)
    out[0:4, :] = total[0:4]

    for d in range(1, sections):
        tap_copy(section_peer(d), me, d).wait_send()
        for p in range(len(parcels)):
            a2a_copy(p, section_peer(d), me, d).wait_send()
    for d in range(1, z_size):
        z_copy(d).wait_send()

    def drain(layer, carry):
        for b in range(blocks):

            @pl.when(q > 0)
            def _():
                halo_copy(layer, b).wait_send()

        for half in range(CORES):

            @pl.when(jnp.logical_not(stays(layer, half)))
            def _():
                msg_copy(layer, half).wait_send()

        return carry

    lax.fori_loop(0, sections, drain, 0)


def adagrad(grad_part, second_part):
    return grad_part / jnp.sqrt(second_part + grad_part * grad_part)


def body(sections, seqs, cotangent, in_gate, mid_gate, layer_inputs, filters, steer_second, filter_second):
    rows, channels = cotangent.shape
    filt_len = filters.shape[1]
    mine = channels // sections
    groups = mine // GROUP
    z_size = seqs // (CORES * Y_PARTS)
    assert rows == filt_len == 128 and mine == 2 * WIDE
    dma = pltpu.SemaphoreType.DMA
    hbm_spec = pl.BlockSpec(memory_space=pltpu.HBM)
    vmem_spec = pl.BlockSpec(memory_space=pltpu.VMEM)
    sums = pl.pallas_call(
        functools.partial(kernel, sections, seqs),
        out_shape=jax.ShapeDtypeStruct((8, 128), F32),
        in_specs=[hbm_spec] * 5,
        out_specs=vmem_spec,
        scratch_shapes=[
            pltpu.VMEM((rows, channels), BF16),
            pltpu.VMEM((rows, channels), BF16),
            pltpu.VMEM((rows, channels), BF16),
            pltpu.VMEM((sections, rows, mine), BF16),
            pltpu.VMEM((sections, rows, mine), BF16),
            pltpu.VMEM((sections, rows, mine), BF16),
            pltpu.VMEM((rows, mine), BF16),
            pltpu.VMEM((filt_len, channels // GROUP), BF16),
            pltpu.VMEM((sections, groups, filt_len), BF16),
            pltpu.VMEM((sections, groups, filt_len), BF16),
            pltpu.VMEM((sections, mine // WIDE, WIDE // GROUP * rows, 2 * rows), BF16),
            pltpu.VMEM((sections, 3 * rows, mine), BF16),
            pltpu.VMEM((rows, rows), BF16),
            pltpu.VMEM((sections, 1, mine), F32),
            pltpu.VMEM((sections, CORES, mine // 128, 8, 128), F32),
            pltpu.VMEM((sections // Y_PARTS, Y_PARTS, CORES, mine // 128, 8, 128), F32),
            pltpu.VMEM((z_size, 8, 128), F32),
            pltpu.VMEM((z_size, 8, 128), F32),
            dma((2,)),
            dma((3,)),
            dma((3, sections)),
            dma((3, sections)),
            dma((sections,)),
            dma((sections,)),
            dma((sections, mine // WIDE)),
            dma((sections, mine // WIDE)),
            dma((sections, CORES)),
            dma((sections // Y_PARTS, Y_PARTS, CORES)),
            dma((z_size,)),
            dma((z_size,)),
        ],
        compiler_params=pltpu.CompilerParams(
            collective_id=0, has_side_effects=True, vmem_limit_bytes=63 * 2**20
        ),
    )(cotangent, in_gate[0], mid_gate[0], layer_inputs[0], filters[0])
    steer_part = sums[4:5, :64]
    filter_part = sums[0:4].T
    return (
        adagrad(steer_part, steer_second),
        adagrad(filter_part, filter_second[0])[None],
    )


def solution(mesh):
    in_specs = (
        P("seq", None),
        P("section", "seq", None),
        P("section", "seq", None),
        P("section", "seq", None),
        P("section", None, None),
        P("section", "seq"),
        P("section", None, "seq"),
    )
    out_specs = (P("section", "seq"), P("section", None, "seq"))
    step = functools.partial(body, mesh.shape["section"], mesh.shape["seq"])
    return jax.shard_map(step, mesh=mesh, in_specs=in_specs, out_specs=out_specs, check_vma=False)
```
